32 devices in a mesh: dp: 4 (over z), seq: 8 (over y, x, core).
Axes of the slice: x: 2, y: 2, z: 4, core: 2. Of those that a mesh axis runs over, the one named last changes fastest.
Arguments:
- patches: bfloat16 [6144, 1280], P(('dp', 'seq')), may hold values from -6 to 6
- query_key_value: bfloat16 [6144, 3840], P(('dp', 'seq')), may hold values from -100 to 100
- counts: int32 [32, 4], P(('dp', 'seq')), may hold values from 4 to 48, as said below
- owner_index: int32 [1536, 1], P(('dp', 'seq')), may hold values from 0 to 7; in each aligned block of 48 rows (0 to 47, 48 to 95, ...) at most 6 rows name the same one
- out_weight: bfloat16 [1280, 1280], P(None, 'dp'), may hold values from -0.15625 to 0.15625
- ln_gain: float32 [1280], replicated, may hold values from 0.25 to 1.75
- ln_bias: float32 [1280], replicated, may hold values from -3 to 3
Outputs:
- image_tokens: bfloat16 [1536, 5120], P(('dp', 'seq'))
The draws below stay inside these ranges and needn't reach their ends.
Inputs may be any that keep to these rules, and one draw needn't show every extreme that they name: Every count is a multiple of 4, each device's counts sum to at most 192, and some device's counts sum to exactly 192. `owner_index`: among the merge groups of one device, at most 6 name the same owner.
All inputs are finite; a program needn't handle non-finite values.
Results may differ from the reference program's by a relative error of at most 0.0029.
Values may be sent and summed in bfloat16 or wider, within the bound.
A program may use at most 64 MiB of HBM per device.

```python
import math
import jax
import jax.numpy as jnp
import numpy as np
from jax import lax

DV = 1280
HEADS = 16
IMGS = 4
PCAP = 192
GROUPS_DEV = 48
CAP = 6
ROWS = 6144
GROUPS = 1536
N_DP = 4
N_SEQ = 8
DEVICES = 32


def draw_counts(key, part):
    per_image = PCAP // (4 * IMGS)
    lowest = max(1, (3 * per_image + 3) // 4)
    group_counts = jax.random.randint(jax.random.fold_in(key, 11), (DEVICES, IMGS), lowest, per_image + 1)
    full_device = jax.random.randint(jax.random.fold_in(key, 13), (), 0, DEVICES)
    device_ids = jnp.arange(DEVICES, dtype=jnp.int32)
    group_counts = jnp.where(device_ids[:, None] == full_device, per_image, group_counts)
    return (4 * group_counts).astype(jnp.int32)


def draw_query_key_value(key, part):
    base = jnp.clip(jax.random.normal(jax.random.fold_in(key, 21), (ROWS, 3 * DV), jnp.float32), -4.0, 4.0)
    return jnp.clip(base, -100.0, 100.0).astype(jnp.bfloat16)


def steps_of(own_key, extent, pieces, low, top_value):
    level, own = 1.0, jax.random.fold_in(own_key, 6)
    for dim, parts in pieces:
        steps = jnp.exp(jax.random.uniform(jax.random.fold_in(own, dim), (parts,), jnp.float32, low / len(pieces), top_value / len(pieces)))
        level = level * jnp.repeat(steps, extent[dim] // parts).reshape([-1 if axis == dim else 1 for axis in range(len(extent))])
    return level


def shared_out(rng, own, number, rows, number_of, top, most, slope):
    ranking = jax.random.permutation(rng, number_of)
    crowded, common = shares(number_of, rows * top, most, slope, True), shares(number_of, rows * top, most, slope, False)
    places = jnp.arange(number_of)

    def named(sizes, turn):
        used = int((sizes > 0).sum())
        fixed = max(1, used // 4)
        shifted = fixed + (places - fixed + turn * (used - fixed)) % max(1, number_of - fixed)
        return jnp.zeros((number_of,), jnp.int32).at[ranking[jnp.where(places < fixed, places, shifted)]].set(jnp.asarray(sizes, jnp.int32))

    sizes = jnp.where(number % 4 == 0, named(crowded, number // 4), named(common, number - number // 4 - 1))
    mixed = jax.random.permutation(jax.random.fold_in(own, 3), number_of)
    giver, taker = mixed[0:number_of // 2 * 2:2], mixed[1:number_of // 2 * 2:2]
    slack = jnp.minimum(sizes[giver] - 1, most - sizes[taker]) // 2
    slack = jnp.where((giver == ranking[0]) | (taker == ranking[0]) | (sizes[taker] == 0), 0, jnp.maximum(slack, 0))
    shifted = jax.random.randint(jax.random.fold_in(own, 4), (number_of // 2,), 0, 1 << 20) % (slack + 1)
    sizes = sizes.at[giver].add(-shifted).at[taker].add(shifted)
    labels = jnp.searchsorted(jnp.cumsum(sizes), jnp.arange(rows * top), side="right").astype(jnp.int32)
    table = labels.reshape(top, rows).T
    table = table[jax.random.permutation(jax.random.fold_in(own, 1), rows)]
    turn = jax.random.randint(jax.random.fold_in(own, 2), (rows, 1), 0, top)
    return jnp.take_along_axis(table, (jnp.arange(top)[None, :] + turn) % top, axis=1)


def shares(number_of, total, bound, skew, full):
    weights = [(1 << 20) // math.isqrt(rank ** skew) + 1 for rank in range(1, number_of + 1)]
    largest = bound if full else min(bound, max(-(-total // number_of), total * weights[0] // sum(weights)))
    least = 1 if total - largest >= number_of - 1 else 0
    given, surplus = [largest] + [least] * (number_of - 1), total - largest - least * (number_of - 1)
    while surplus > 0:
        free = [i for i in range(1, number_of) if given[i] < largest] or [i for i in range(1, number_of) if given[i] < bound]
        whole, budget = sum([weights[i] for i in free]), surplus
        for i in free:
            more = min(bound - given[i], max(1, budget * weights[i] // whole), surplus)
            given[i] = given[i] + more
            surplus = surplus - more
    return np.array(given)


def scatter_about(key, dims, width, reach, cuts=(), kind=jnp.bfloat16):
    array = width * jax.random.normal(key, dims, jnp.float32)
    if cuts:
        array = array * steps_of(key, dims, cuts, -0.22, 0.18)
    return jnp.clip(array, -reach, reach).astype(kind)


def setup_inputs(seed: int = 0) -> dict:
    seeds = jax.random.split(jax.random.key(seed), 8)
    patches = scatter_about(seeds[0], (ROWS, DV), 1.0, 6.0, ((0, 32),))
    query_key_value = draw_query_key_value(jax.random.fold_in(seeds[7], 71), 0)
    counts = draw_counts(jax.random.fold_in(seeds[7], 71), 0)
    owner_index_keys = jax.random.split(jax.random.fold_in(seeds[3], 1), GROUPS // GROUPS_DEV)
    owner_index_turns = jax.random.permutation(jax.random.fold_in(seeds[3], 3), GROUPS // GROUPS_DEV)
    owner_index = jax.vmap(lambda own, number: shared_out(jax.random.fold_in(seeds[3], 2), own, number, GROUPS_DEV, N_SEQ, 1, CAP, 1))(owner_index_keys, owner_index_turns).reshape((GROUPS, 1))
    out_weight = scatter_about(seeds[4], (DV, DV), DV ** -0.5, 0.15625, ((1, 4),))
    ln_gain = jnp.clip(1.0 + 0.15 * jax.random.normal(seeds[5], (DV,), jnp.float32), 0.25, 1.75)
    ln_bias = scatter_about(seeds[6], (DV,), 0.5, 3.0, (), jnp.float32)
    return {"patches": patches, "query_key_value": query_key_value, "counts": counts, "owner_index": owner_index, "out_weight": out_weight, "ln_gain": ln_gain, "ln_bias": ln_bias}


def segment_rows(count_row, row_count):
    image_ends = jnp.cumsum(count_row.astype(jnp.int32))
    row_ids = jnp.arange(row_count, dtype=jnp.int32)
    return lax.optimization_barrier(jnp.sum((row_ids[:, None] >= image_ends[None, :]).astype(jnp.int32), axis=1))

def attend(packed, segment_ids, model_width):
    row_count = packed.shape[0]
    head_size = model_width // HEADS
    queries = packed[:, :model_width].astype(jnp.float32).reshape(row_count, HEADS, head_size)
    keys_all = packed[:, model_width:2 * model_width].astype(jnp.float32).reshape(row_count, HEADS, head_size)
    values_all = packed[:, 2 * model_width:].astype(jnp.float32).reshape(row_count, HEADS, head_size)
    scores = jnp.einsum('qhd,khd->hqk', queries, keys_all) * head_size ** (-0.5)
    same_image = segment_ids[:, None] == segment_ids[None, :]
    scores = jnp.where(same_image[None, :, :], scores, -1e+30)
    top_score = lax.optimization_barrier(jnp.max(scores, axis=2, keepdims=True))
    expo = jnp.exp(scores - top_score)
    attn_weights = (expo / lax.optimization_barrier(jnp.sum(expo, axis=2, keepdims=True))).astype(jnp.bfloat16)
    context = jnp.einsum('hqk,khd->qhd', attn_weights.astype(jnp.float32), values_all)
    return context.reshape(row_count, model_width).astype(jnp.bfloat16)

def merge_and_place(hidden, segment_ids, owners, ln_gain, ln_bias, owner_count, capacity):
    row_count, model_width = hidden.shape
    row_mean = lax.optimization_barrier(jnp.mean(hidden, axis=1, keepdims=True))
    centered = hidden - row_mean
    row_var = lax.optimization_barrier(jnp.mean(centered * centered, axis=1, keepdims=True))
    normed = (centered * lax.rsqrt(row_var + 1e-06) * ln_gain[None, :] + ln_bias[None, :]).astype(jnp.bfloat16)
    merged = normed.reshape(row_count // 4, 4 * model_width)
    live_group = segment_ids.reshape(row_count // 4, 4)[:, 0] < IMGS
    group_ids = jnp.arange(row_count // 4, dtype=jnp.int32)
    earlier = (owners[None, :] == owners[:, None]) & (group_ids[None, :] < group_ids[:, None]) & live_group[None, :]
    slot_index = lax.optimization_barrier(jnp.sum(earlier.astype(jnp.int32), axis=1))
    target = owners * capacity + slot_index
    slot_ids = jnp.arange(owner_count * capacity, dtype=jnp.int32)
    onehot_map = ((slot_ids[:, None] == target[None, :]) & live_group[None, :]).astype(jnp.bfloat16)
    return jnp.dot(onehot_map, merged, preferred_element_type=jnp.float32).astype(jnp.bfloat16)

def reference(patches, query_key_value, counts, owner_index, out_weight, ln_gain, ln_bias):
    model_width = patches.shape[1]
    device_count = counts.shape[0]
    patch_blocks = patches.reshape(device_count, PCAP, model_width)
    packed_blocks = query_key_value.reshape(device_count, PCAP, 3 * model_width)
    owner_blocks = owner_index.reshape(device_count, PCAP // 4)

    def one_device(inputs):
        patch_rows, packed, count_row, owners = inputs
        segment_ids = segment_rows(count_row, PCAP)
        context = attend(packed, segment_ids, model_width)
        hidden = patch_rows.astype(jnp.float32) + jnp.dot(context, out_weight, preferred_element_type=jnp.float32)
        return merge_and_place(hidden, segment_ids, owners, ln_gain, ln_bias, N_SEQ, CAP)
    outgoing = lax.map(one_device, (patch_blocks, packed_blocks, counts, owner_blocks))
    outgoing = outgoing.reshape(N_DP, N_SEQ, N_SEQ, CAP, 4 * model_width)
    outgoing = jnp.transpose(outgoing, (0, 2, 1, 3, 4))
    return outgoing.reshape(device_count * N_SEQ * CAP, 4 * model_width)
```

```python
import functools

import jax
import jax.numpy as jnp
from jax import lax
from jax.experimental import pallas as pl
from jax.experimental.pallas import tpu as pltpu
from jax.sharding import PartitionSpec as P

HEADS = 16
IMGS = 4
MESH = pl.DeviceIdType.MESH


def segment_rows(count_row, row_count):
    image_ends = jnp.cumsum(count_row)
    row_ids = jnp.arange(row_count, dtype=jnp.int32)
    return jnp.sum((row_ids[:, None] >= image_ends[None, :]).astype(jnp.int32), axis=1)


def attend(packed, segment_ids, model_width):
    row_count = packed.shape[0]
    head_size = model_width // HEADS
    queries = packed[:, :model_width].reshape(row_count, HEADS, head_size)
    keys_all = packed[:, model_width : 2 * model_width].reshape(row_count, HEADS, head_size)
    values_all = packed[:, 2 * model_width :].reshape(row_count, HEADS, head_size)
    scores = jnp.einsum(
        "qhd,khd->hqk", queries, keys_all, preferred_element_type=jnp.float32
    ) * head_size ** (-0.5)
    same_image = segment_ids[:, None] == segment_ids[None, :]
    scores = jnp.where(same_image[None, :, :], scores, -1e30)
    top_score = jnp.max(scores, axis=2, keepdims=True)
    expo = jnp.exp(scores - top_score)
    attn_weights = (expo / jnp.sum(expo, axis=2, keepdims=True)).astype(jnp.bfloat16)
    context = jnp.einsum(
        "hqk,khd->qhd", attn_weights, values_all, preferred_element_type=jnp.float32
    )
    return context.reshape(row_count, model_width).astype(jnp.bfloat16)


def merge_and_place(hidden, segment_ids, owners, ln_gain, ln_bias, owner_count, capacity):
    row_count, model_width = hidden.shape
    row_mean = jnp.mean(hidden, axis=1, keepdims=True)
    centered = hidden - row_mean
    row_var = jnp.mean(centered * centered, axis=1, keepdims=True)
    normed = (centered * lax.rsqrt(row_var + 1e-06) * ln_gain[None, :] + ln_bias[None, :]).astype(
        jnp.bfloat16
    )
    merged = normed.reshape(row_count // 4, 4 * model_width)
    live_group = segment_ids.reshape(row_count // 4, 4)[:, 0] < IMGS
    group_ids = jnp.arange(row_count // 4, dtype=jnp.int32)
    earlier = (
        (owners[None, :] == owners[:, None])
        & (group_ids[None, :] < group_ids[:, None])
        & live_group[None, :]
    )
    slot_index = jnp.sum(earlier.astype(jnp.int32), axis=1)
    target = owners * capacity + slot_index
    slot_ids = jnp.arange(owner_count * capacity, dtype=jnp.int32)
    onehot_map = ((slot_ids[:, None] == target[None, :]) & live_group[None, :]).astype(jnp.bfloat16)
    return jnp.dot(onehot_map, merged, preferred_element_type=jnp.float32).astype(jnp.bfloat16)


def plain_body(patches, query_key_value, counts, owner_index, out_weight, ln_gain, ln_bias):
    row_count, model_width = patches.shape
    owner_count = lax.axis_size("seq")
    group_count = row_count // 4
    capacity = max(2, (group_count + owner_count - 1) // owner_count)
    segment_ids = segment_rows(counts[0], row_count)
    context = attend(query_key_value, segment_ids, model_width)
    slice_rows = model_width // owner_count
    own_slice = lax.dynamic_slice_in_dim(
        out_weight, lax.axis_index("seq") * slice_rows, slice_rows, 0
    )
    weight_slab = lax.all_gather(own_slice, "dp", axis=1, tiled=True)
    projected = jnp.dot(
        context,
        lax.all_gather(weight_slab, "seq", axis=0, tiled=True),
        preferred_element_type=jnp.float32,
    )
    hidden = patches.astype(jnp.float32) + projected
    outgoing = merge_and_place(
        hidden, segment_ids, owner_index[:, 0], ln_gain, ln_bias, owner_count, capacity
    )
    outgoing = outgoing.reshape(owner_count, capacity, 4 * model_width)
    received = lax.all_to_all(outgoing, "seq", split_axis=0, concat_axis=0, tiled=True)
    return received.reshape(owner_count * capacity, 4 * model_width)


def flip(index, mask):
    bit = 1
    while bit <= mask:
        if mask & bit:
            index = index + bit - 2 * bit * ((index // bit) % 2)
        bit *= 2
    return index


def iota(shape, dim):
    return lax.broadcasted_iota(jnp.int32, shape, dim)


def fused_kernel(
    n_dp, n_seq, capacity,
    patches_ref, packed_ref, counts_ref, owners_ref, weight_ref, gain_ref, bias_ref,
    landed_ref,
    patches_v, packed_v, weight_v, context_v, outgoing_v,
    local_sem, z_send, z_recv, p_send, p_recv, f_send, f_recv, a_send, a_recv,
):
    row_count, model_width = patches_ref.shape
    head_size = model_width // HEADS
    piece_rows = weight_ref.shape[0] // (n_seq // 2)
    piece_lanes = model_width // 2
    my_dp, my_seq = lax.axis_index("dp"), lax.axis_index("seq")
    plane = list(range(2, n_seq, 2))
    partner = flip(my_seq, 1)

    load_packed = pltpu.make_async_copy(packed_ref, packed_v, local_sem.at[0])
    load_patches = pltpu.make_async_copy(patches_ref, patches_v, local_sem.at[1])
    load_weight = pltpu.make_async_copy(weight_ref, weight_v.at[my_dp], local_sem.at[2])
    load_packed.start()
    load_weight.start()
    load_patches.start()

    barrier = pltpu.get_barrier_semaphore()
    for k in range(1, n_dp):
        pl.semaphore_signal(
            barrier, inc=1, device_id=(lax.rem(my_dp + k, n_dp), my_seq), device_id_type=MESH
        )
    for m in range(1, n_seq):
        pl.semaphore_signal(barrier, inc=1, device_id=(my_dp, flip(my_seq, m)), device_id_type=MESH)
    pl.semaphore_wait(barrier, n_dp + n_seq - 2)

    def piece_of(ref, seq):
        return ref.at[
            pl.ds(pl.multiple_of((seq // 2) * piece_rows, piece_rows), piece_rows),
            pl.ds(pl.multiple_of((seq % 2) * piece_lanes, piece_lanes), piece_lanes),
        ]

    z_copies = []
    for k in range(1, n_dp):
        copy = pltpu.make_async_remote_copy(
            src_ref=piece_of(weight_ref, my_seq),
            dst_ref=piece_of(weight_v.at[my_dp], my_seq),
            send_sem=z_send.at[k - 1],
            recv_sem=z_recv.at[k - 1],
            device_id=(lax.rem(my_dp + k, n_dp), my_seq),
            device_id_type=MESH,
        )
        copy.start()
        z_copies.append(copy)

    def piece_copy(k, seq_of_rows, target, send_sem, recv_sem):
        piece = piece_of(weight_v.at[lax.rem(my_dp + n_dp - k, n_dp)], seq_of_rows)
        return pltpu.make_async_remote_copy(
            src_ref=piece, dst_ref=piece, send_sem=send_sem, recv_sem=recv_sem,
            device_id=(my_dp, target), device_id_type=MESH,
        )

    p_copies, f_copies = {}, {}

    def spread(k):
        z_copies[k - 1].wait_recv()
        for i, m in enumerate(plane + [1]):
            copy = piece_copy(
                k, my_seq, flip(my_seq, m), p_send.at[k - 1, i], p_recv.at[k - 1, i]
            )
            copy.start()
            p_copies[k, i] = copy

    def forward(k, i):
        p_copies[k, i].wait_recv()
        copy = piece_copy(
            k, flip(my_seq, plane[i]), partner, f_send.at[k - 1, i], f_recv.at[k - 1, i]
        )
        copy.start()
        f_copies[k, i] = copy

    hooks = [functools.partial(spread, k) for k in range(1, n_dp)]

    load_packed.wait()
    ends, total = [], 0
    for i in range(IMGS):
        total = total + counts_ref[0, i]
        ends.append(total)

    def segments(shape, dim):
        ids = iota(shape, dim)
        found = jnp.zeros(shape, jnp.int32)
        for end in ends:
            found = found + (ids >= end).astype(jnp.int32)
        return found

    same = segments((row_count, row_count), 0) == segments((row_count, row_count), 1)
    scale = head_size ** (-0.5)
    pending = None
    pending_at = 0
    for head in range(HEADS):
        first, last = head * head_size, (head + 1) * head_size
        low, high = first // 128 * 128, -(-last // 128) * 128
        lanes = iota((row_count, high - low), 1)
        mine = (lanes >= first - low) & (lanes < last - low)
        queries = packed_v[:, low:high]
        queries = jnp.where(mine, queries, jnp.zeros_like(queries))
        scores = lax.dot_general(
            queries, packed_v[:, model_width + low : model_width + high],
            (((1,), (1,)), ((), ())), preferred_element_type=jnp.float32,
        )
        scores = jnp.where(same, scores, -1e30)
        top_score = jnp.max(scores, axis=1, keepdims=True)
        expo = jnp.exp((scores - top_score) * scale)
        weights = (expo * (1.0 / jnp.sum(expo, axis=1, keepdims=True))).astype(jnp.bfloat16)
        found = jnp.dot(
            weights, packed_v[:, 2 * model_width + low : 2 * model_width + high],
            preferred_element_type=jnp.float32,
        )
        found = jnp.where(mine, found, 0.0)
        if pending is not None and pending_at > low:
            shared = pending_at - low
            if shared > 0:
                head_part = pending + found[:, :shared]
                found = (
                    jnp.concatenate([head_part, found[:, shared:]], axis=1)
                    if shared < high - low else head_part
                )
        done = last // 128 * 128
        if done > low:
            context_v[:, low:done] = found[:, : done - low].astype(jnp.bfloat16)
        if done < high:
            pending, pending_at = found[:, done - low :], high
        else:
            pending = None
        if hooks and head % 3 == 2:
            hooks.pop(0)()
    while hooks:
        hooks.pop(0)()
    for k in range(1, n_dp):
        for i in range(len(plane)):
            forward(k, i)

    load_weight.wait()
    load_patches.wait()
    for k in range(1, n_dp):
        p_copies[k, len(plane)].wait_recv()
        for i in range(len(plane)):
            f_copies[k, i].wait_recv()
    context = context_v[...]
    hidden = patches_v[...].astype(jnp.float32) + jnp.concatenate(
        [
            lax.dot_general(
                context, weight_v[d], (((1,), (1,)), ((), ())),
                preferred_element_type=jnp.float32,
            )
            for d in range(n_dp)
        ],
        axis=1,
    )
    row_mean = jnp.mean(hidden, axis=1, keepdims=True)
    centered = hidden - row_mean
    row_var = jnp.mean(centered * centered, axis=1, keepdims=True)
    normed = (
        centered * lax.rsqrt(row_var + 1e-06) * gain_ref[...].reshape(1, model_width)
        + bias_ref[...].reshape(1, model_width)
    ).astype(jnp.bfloat16)

    group_count = row_count // 4
    diagonal = iota((group_count, group_count), 0) == iota((group_count, group_count), 1)
    owners = jnp.sum(jnp.where(diagonal, owners_ref[...], 0), axis=1, keepdims=True)
    groups = iota((group_count, row_count), 0)
    group_of_row = iota((group_count, row_count), 1) >> 2
    owner_of_row = jnp.sum(jnp.where(groups == group_of_row, owners, 0), axis=0, keepdims=True)
    earlier = (owners == owner_of_row) & (groups < group_of_row) & (groups * 4 < total)
    slot_of_row = jnp.sum(earlier.astype(jnp.int32), axis=0, keepdims=True)
    block_rows = 4 * capacity
    row_ids = iota((1, row_count), 1)
    place = owner_of_row * block_rows + slot_of_row * 4 + (row_ids & 3)
    place = jnp.where((row_ids >> 2) * 4 < total, place, -1)
    tall = n_seq * 16
    lines = iota((tall, row_count), 0)
    half = model_width // 2
    for f in range(block_rows // 16):
        chosen = ((lines >> 4) * block_rows + 16 * f + (lines & 15) == place).astype(jnp.bfloat16)
        placed = jnp.dot(chosen, normed, preferred_element_type=jnp.float32).astype(jnp.bfloat16)
        outgoing_v[:, :, f * model_width : (f + 1) * model_width] = placed.reshape(
            n_seq, 16, model_width
        )
    if block_rows % 16:
        f = block_rows // 16
        chosen = ((lines >> 4) * block_rows + 16 * f + (lines & 7) == place).astype(jnp.bfloat16)
        placed = jnp.dot(chosen, normed, preferred_element_type=jnp.float32)
        upper = (iota((tall, half), 0) & 15) < 8
        placed = jnp.where(upper, placed[:, :half], placed[:, half:]).astype(jnp.bfloat16)
        outgoing_v[:, :, f * model_width :] = placed.reshape(n_seq, 16, half)

    a_copies = []
    for m in plane[::-1] + [0] + [m + 1 for m in plane[::-1]] + [1]:
        target = flip(my_seq, m)
        if m == 0:
            continue
        copy = pltpu.make_async_remote_copy(
            src_ref=outgoing_v.at[target],
            dst_ref=landed_ref.at[my_seq],
            send_sem=a_send.at[m - 1],
            recv_sem=a_recv.at[m - 1],
            device_id=(my_dp, target),
            device_id_type=MESH,
        )
        copy.start()
        a_copies.append(copy)
    keep = pltpu.make_async_copy(outgoing_v.at[my_seq], landed_ref.at[my_seq], local_sem.at[3])
    keep.start()
    for copy in z_copies + list(p_copies.values()) + list(f_copies.values()):
        copy.wait_send()
    keep.wait()
    for copy in a_copies:
        copy.wait()


def layout_kernel(capacity, landed_ref, out_ref):
    n_seq, _, lanes = landed_ref.shape
    model_width = out_ref.shape[1] // 4
    half = model_width // 2
    block_rows = 4 * capacity
    out_rows = n_seq * capacity
    landed = landed_ref[...].reshape(n_seq * 16, lanes)
    rows = iota((out_rows, n_seq * 16), 0)
    lines = iota((out_rows, n_seq * 16), 1)
    full = block_rows // 16

    def pick(first, line, j, keep):
        spot = first + line
        return (
            (rows == (lines >> 4) * capacity + (spot >> 2)) & ((spot & 3) == j) & keep
        ).astype(jnp.bfloat16)

    always = lines >= 0
    for j in range(4):
        left = jnp.zeros((out_rows, half), jnp.float32)
        right = jnp.zeros((out_rows, half), jnp.float32)
        for f in range(full):
            part = jnp.dot(
                pick(16 * f, lines & 15, j, always),
                landed[:, f * model_width : (f + 1) * model_width],
                preferred_element_type=jnp.float32,
            )
            left, right = left + part[:, :half], right + part[:, half:]
        if block_rows % 16:
            tail = landed[:, full * model_width :]
            left = left + jnp.dot(
                pick(16 * full, lines & 7, j, (lines & 15) < 8), tail,
                preferred_element_type=jnp.float32,
            )
            right = right + jnp.dot(
                pick(16 * full, lines & 7, j, (lines & 15) >= 8), tail,
                preferred_element_type=jnp.float32,
            )
        out_ref[:, j * model_width : j * model_width + half] = left.astype(jnp.bfloat16)
        out_ref[:, j * model_width + half : (j + 1) * model_width] = right.astype(jnp.bfloat16)


def fused_body(patches, query_key_value, counts, owner_index, out_weight, ln_gain, ln_bias):
    row_count, model_width = patches.shape
    n_dp, n_seq = lax.axis_size("dp"), lax.axis_size("seq")
    capacity = max(2, (row_count // 4 + n_seq - 1) // n_seq)
    planes = n_seq // 2 - 1
    block_lanes = model_width * 4 * capacity // 16
    any_spec = pl.BlockSpec(memory_space=pl.ANY)
    vmem_spec = pl.BlockSpec(memory_space=pltpu.VMEM)
    dma = pltpu.SemaphoreType.DMA
    landed = pl.pallas_call(
        functools.partial(fused_kernel, n_dp, n_seq, capacity),
        out_shape=jax.ShapeDtypeStruct((n_seq, 16, block_lanes), jnp.bfloat16),
        in_specs=[
            any_spec, any_spec, pl.BlockSpec(memory_space=pltpu.SMEM), vmem_spec, any_spec,
            vmem_spec, vmem_spec,
        ],
        out_specs=vmem_spec,
        scratch_shapes=[
            pltpu.VMEM(patches.shape, jnp.bfloat16),
            pltpu.VMEM(query_key_value.shape, jnp.bfloat16),
            pltpu.VMEM((n_dp,) + out_weight.shape[::-1], jnp.bfloat16),
            pltpu.VMEM(patches.shape, jnp.bfloat16),
            pltpu.VMEM((n_seq, 16, block_lanes), jnp.bfloat16),
            dma((4,)),
            dma((n_dp - 1,)), dma((n_dp - 1,)),
            dma((n_dp - 1, planes + 1)), dma((n_dp - 1, planes + 1)),
            dma((n_dp - 1, planes)), dma((n_dp - 1, planes)),
            dma((n_seq - 1,)), dma((n_seq - 1,)),
        ],
        compiler_params=pltpu.CompilerParams(
            collective_id=0, has_side_effects=True
        ),
        name="fused",
    )(
        patches, query_key_value, counts, owner_index.T, out_weight.T,
        ln_gain, ln_bias,
    )
    return pl.pallas_call(
        functools.partial(layout_kernel, capacity),
        out_shape=jax.ShapeDtypeStruct((n_seq * capacity, 4 * model_width), jnp.bfloat16),
        in_specs=[vmem_spec],
        out_specs=vmem_spec,
        compiler_params=pltpu.CompilerParams(vmem_limit_bytes=16 * 1024 * 1024),
        name="layout",
    )(landed)


def body(patches, query_key_value, counts, owner_index, out_weight, ln_gain, ln_bias):
    n_seq = lax.axis_size("seq")
    whole_tiles = out_weight.shape[1] % (8 * n_seq) == 0 and n_seq & (n_seq - 1) == 0
    run = fused_body if whole_tiles else plain_body
    return run(patches, query_key_value, counts, owner_index, out_weight, ln_gain, ln_bias)


def solution(mesh):
    placed = (
        P(("dp", "seq"), None),
        P(("dp", "seq"), None),
        P(("dp", "seq"), None),
        P(("dp", "seq"), None),
        P(None, "dp"),
        P(),
        P(),
    )
    return jax.shard_map(
        body, mesh=mesh, in_specs=placed, out_specs=P(("dp", "seq"), None), check_vma=False
    )
```

```python
import functools

import jax
import jax.numpy as jnp
from jax import lax
from jax.experimental import pallas as pl
from jax.experimental.pallas import tpu as pltpu
from jax.sharding import PartitionSpec as P

HEADS = 16
IMGS = 4
MESH = pl.DeviceIdType.MESH


def segment_rows(count_row, row_count):
    image_ends = jnp.cumsum(count_row)
    row_ids = jnp.arange(row_count, dtype=jnp.int32)
    return jnp.sum((row_ids[:, None] >= image_ends[None, :]).astype(jnp.int32), axis=1)


def attend(packed, segment_ids, model_width):
    row_count = packed.shape[0]
    head_size = model_width // HEADS
    queries = packed[:, :model_width].reshape(row_count, HEADS, head_size)
    keys_all = packed[:, model_width : 2 * model_width].reshape(row_count, HEADS, head_size)
    values_all = packed[:, 2 * model_width :].reshape(row_count, HEADS, head_size)
    scores = jnp.einsum(
        "qhd,khd->hqk", queries, keys_all, preferred_element_type=jnp.float32
    ) * head_size ** (-0.5)
    same_image = segment_ids[:, None] == segment_ids[None, :]
    scores = jnp.where(same_image[None, :, :], scores, -1e30)
    top_score = jnp.max(scores, axis=2, keepdims=True)
    expo = jnp.exp(scores - top_score)
    attn_weights = (expo / jnp.sum(expo, axis=2, keepdims=True)).astype(jnp.bfloat16)
    context = jnp.einsum(
        "hqk,khd->qhd", attn_weights, values_all, preferred_element_type=jnp.float32
    )
    return context.reshape(row_count, model_width).astype(jnp.bfloat16)


def merge_and_place(hidden, segment_ids, owners, ln_gain, ln_bias, owner_count, capacity):
    row_count, model_width = hidden.shape
    row_mean = jnp.mean(hidden, axis=1, keepdims=True)
    centered = hidden - row_mean
    row_var = jnp.mean(centered * centered, axis=1, keepdims=True)
    normed = (centered * lax.rsqrt(row_var + 1e-06) * ln_gain[None, :] + ln_bias[None, :]).astype(
        jnp.bfloat16
    )
    merged = normed.reshape(row_count // 4, 4 * model_width)
    live_group = segment_ids.reshape(row_count // 4, 4)[:, 0] < IMGS
    group_ids = jnp.arange(row_count // 4, dtype=jnp.int32)
    earlier = (
        (owners[None, :] == owners[:, None])
        & (group_ids[None, :] < group_ids[:, None])
        & live_group[None, :]
    )
    slot_index = jnp.sum(earlier.astype(jnp.int32), axis=1)
    target = owners * capacity + slot_index
    slot_ids = jnp.arange(owner_count * capacity, dtype=jnp.int32)
    onehot_map = ((slot_ids[:, None] == target[None, :]) & live_group[None, :]).astype(jnp.bfloat16)
    return jnp.dot(onehot_map, merged, preferred_element_type=jnp.float32).astype(jnp.bfloat16)


def plain_body(patches, query_key_value, counts, owner_index, out_weight, ln_gain, ln_bias):
    row_count, model_width = patches.shape
    owner_count = lax.axis_size("seq")
    group_count = row_count // 4
    capacity = max(2, (group_count + owner_count - 1) // owner_count)
    segment_ids = segment_rows(counts[0], row_count)
    context = attend(query_key_value, segment_ids, model_width)
    slice_rows = model_width // owner_count
    own_slice = lax.dynamic_slice_in_dim(
        out_weight, lax.axis_index("seq") * slice_rows, slice_rows, 0
    )
    weight_slab = lax.all_gather(own_slice, "dp", axis=1, tiled=True)
    projected = jnp.dot(
        context,
        lax.all_gather(weight_slab, "seq", axis=0, tiled=True),
        preferred_element_type=jnp.float32,
    )
    hidden = patches.astype(jnp.float32) + projected
    outgoing = merge_and_place(
        hidden, segment_ids, owner_index[:, 0], ln_gain, ln_bias, owner_count, capacity
    )
    outgoing = outgoing.reshape(owner_count, capacity, 4 * model_width)
    received = lax.all_to_all(outgoing, "seq", split_axis=0, concat_axis=0, tiled=True)
    return received.reshape(owner_count * capacity, 4 * model_width)


def flip(index, mask):
    bit = 1
    while bit <= mask:
        if mask & bit:
            index = index + bit - 2 * bit * ((index // bit) % 2)
        bit *= 2
    return index


def iota(shape, dim):
    return lax.broadcasted_iota(jnp.int32, shape, dim)


def fused_kernel(
    n_dp, n_seq, capacity,
    patches_ref, packed_ref, counts_ref, owners_ref, weight_ref, gain_ref, bias_ref,
    landed_ref,
    patches_v, packed_v, weight_v, context_v, projected_v, outgoing_v,
    local_sem, z_send, z_recv, p_send, p_recv, a_send, a_recv,
):
    row_count, model_width = patches_ref.shape
    head_size = model_width // HEADS
    piece_rows = weight_ref.shape[0] // (n_seq // 2)
    piece_lanes = model_width // 2
    my_dp, my_seq = lax.axis_index("dp"), lax.axis_index("seq")
    plane = list(range(2, n_seq, 2))
    partner = flip(my_seq, 1)

    load_packed = pltpu.make_async_copy(packed_ref, packed_v, local_sem.at[0])
    load_patches = pltpu.make_async_copy(patches_ref, patches_v, local_sem.at[1])
    load_weight = pltpu.make_async_copy(weight_ref, weight_v.at[my_dp], local_sem.at[2])
    load_packed.start()
    load_weight.start()
    load_patches.start()

    barrier = pltpu.get_barrier_semaphore()
    for k in range(1, n_dp):
        pl.semaphore_signal(
            barrier, inc=1, device_id=(lax.rem(my_dp + k, n_dp), my_seq), device_id_type=MESH
        )
    for m in range(1, n_seq):
        pl.semaphore_signal(barrier, inc=1, device_id=(my_dp, flip(my_seq, m)), device_id_type=MESH)
    pl.semaphore_wait(barrier, n_dp + n_seq - 2)

    def piece_of(ref, seq):
        return ref.at[
            pl.ds(pl.multiple_of((seq // 2) * piece_rows, piece_rows), piece_rows),
            pl.ds(pl.multiple_of((seq % 2) * piece_lanes, piece_lanes), piece_lanes),
        ]

    def at_dp(table):
        return sum(
            entry * (1 - ((my_dp - i + n_dp) % n_dp + n_dp - 1) // n_dp)
            for i, entry in enumerate(table)
        )

    orders = [
        sorted((e for e in range(n_dp) if e != d), key=lambda e: (abs(e - d), e))
        for d in range(n_dp)
    ]
    rounds = range(n_dp - 1)
    sources = [at_dp([order[r] for order in orders]) for r in rounds]
    core = my_seq % 2
    x_side, y_side = flip(my_seq, 2), flip(my_seq, 4)
    side_a = (1 - core) * x_side + core * y_side
    side_b = core * x_side + (1 - core) * y_side
    far_side = flip(my_seq, 6)

    def z_copy(r, owner_dp):
        return pltpu.make_async_remote_copy(
            src_ref=piece_of(weight_ref, my_seq),
            dst_ref=piece_of(weight_v.at[owner_dp], my_seq),
            send_sem=z_send.at[r],
            recv_sem=z_recv.at[owner_dp],
            device_id=(sources[r], my_seq),
            device_id_type=MESH,
        )

    z_copies = [z_copy(r, my_dp) for r in rounds]
    for copy in z_copies:
        copy.start()

    sent = {}

    def send_piece(r, kind, seq_of_rows, target):
        piece = piece_of(weight_v.at[sources[r]], seq_of_rows)
        copy = pltpu.make_async_remote_copy(
            src_ref=piece, dst_ref=piece, send_sem=p_send.at[r, kind], recv_sem=p_recv.at[r, kind],
            device_id=(my_dp, target), device_id_type=MESH,
        )
        copy.start()
        sent[r, kind] = copy

    def from_z(r):
        z_copy(r, sources[r]).wait_recv()
        send_piece(r, 0, my_seq, side_a)
        send_piece(r, 1, my_seq, side_b)
        send_piece(r, 3, my_seq, partner)

    def from_sides(r):
        sent[r, 0].wait_recv()
        send_piece(r, 2, side_a, side_b)
        send_piece(r, 4, side_a, partner)
        sent[r, 1].wait_recv()
        send_piece(r, 5, side_b, partner)

    def from_far(r):
        sent[r, 2].wait_recv()
        send_piece(r, 6, far_side, partner)

    def project(dp):
        projected_v[dp] = lax.dot_general(
            context_v[...], weight_v[dp], (((1,), (1,)), ((), ())),
            preferred_element_type=jnp.float32,
        )

    def finish(r):
        for kind in range(3, 7):
            sent[r, kind].wait_recv()
        project(sources[r])

    load_packed.wait()
    ends, total = [], 0
    for i in range(IMGS):
        total = total + counts_ref[0, i]
        ends.append(total)

    def segments(shape, dim):
        ids = iota(shape, dim)
        found = jnp.zeros(shape, jnp.int32)
        for end in ends:
            found = found + (ids >= end).astype(jnp.int32)
        return found

    same = segments((row_count, row_count), 0) == segments((row_count, row_count), 1)
    scale = head_size ** (-0.5)
    pending = None
    pending_at = 0
    for head in range(HEADS):
        first, last = head * head_size, (head + 1) * head_size
        low, high = first // 128 * 128, -(-last // 128) * 128
        lanes = iota((row_count, high - low), 1)
        mine = (lanes >= first - low) & (lanes < last - low)
        queries = packed_v[:, low:high]
        queries = jnp.where(mine, queries, jnp.zeros_like(queries))
        scores = lax.dot_general(
            queries, packed_v[:, model_width + low : model_width + high],
            (((1,), (1,)), ((), ())), preferred_element_type=jnp.float32,
        )
        scores = jnp.where(same, scores, -1e30)
        top_score = jnp.max(scores, axis=1, keepdims=True)
        expo = jnp.exp((scores - top_score) * scale)
        weights = (expo * (1.0 / jnp.sum(expo, axis=1, keepdims=True))).astype(jnp.bfloat16)
        found = jnp.dot(
            weights, packed_v[:, 2 * model_width + low : 2 * model_width + high],
            preferred_element_type=jnp.float32,
        )
        found = jnp.where(mine, found, 0.0)
        if pending is not None and pending_at > low:
            shared = pending_at - low
            if shared > 0:
                head_part = pending + found[:, :shared]
                found = (
                    jnp.concatenate([head_part, found[:, shared:]], axis=1)
                    if shared < high - low else head_part
                )
        done = last // 128 * 128
        if done > low:
            context_v[:, low:done] = found[:, : done - low].astype(jnp.bfloat16)
        if done < high:
            pending, pending_at = found[:, done - low :], high
        else:
            pending = None

    load_weight.wait()
    project(my_dp)
    load_patches.wait()
    for step in range(n_dp + 2):
        if step < n_dp - 1:
            from_z(step)
        if 1 <= step < n_dp:
            from_sides(step - 1)
        if 2 <= step < n_dp + 1:
            from_far(step - 2)
        if 3 <= step:
            finish(step - 3)
    hidden = patches_v[...].astype(jnp.float32) + jnp.concatenate(
        [projected_v[d] for d in range(n_dp)], axis=1
    )
    row_mean = jnp.mean(hidden, axis=1, keepdims=True)
    centered = hidden - row_mean
    row_var = jnp.mean(centered * centered, axis=1, keepdims=True)
    normed = (
        centered * lax.rsqrt(row_var + 1e-06) * gain_ref[...].reshape(1, model_width)
        + bias_ref[...].reshape(1, model_width)
    ).astype(jnp.bfloat16)

    group_count = row_count // 4
    diagonal = iota((group_count, group_count), 0) == iota((group_count, group_count), 1)
    owners = jnp.sum(jnp.where(diagonal, owners_ref[...], 0), axis=1, keepdims=True)
    groups = iota((group_count, row_count), 0)
    group_of_row = iota((group_count, row_count), 1) >> 2
    owner_of_row = jnp.sum(jnp.where(groups == group_of_row, owners, 0), axis=0, keepdims=True)
    earlier = (owners == owner_of_row) & (groups < group_of_row) & (groups * 4 < total)
    slot_of_row = jnp.sum(earlier.astype(jnp.int32), axis=0, keepdims=True)
    block_rows = 4 * capacity
    row_ids = iota((1, row_count), 1)
    place = owner_of_row * block_rows + slot_of_row * 4 + (row_ids & 3)
    place = jnp.where((row_ids >> 2) * 4 < total, place, -1)
    tall = n_seq * 16
    lines = iota((tall, row_count), 0)
    half = model_width // 2
    for f in range(block_rows // 16):
        chosen = ((lines >> 4) * block_rows + 16 * f + (lines & 15) == place).astype(jnp.bfloat16)
        placed = jnp.dot(chosen, normed, preferred_element_type=jnp.float32).astype(jnp.bfloat16)
        outgoing_v[:, :, f * model_width : (f + 1) * model_width] = placed.reshape(
            n_seq, 16, model_width
        )
    if block_rows % 16:
        f = block_rows // 16
        chosen = ((lines >> 4) * block_rows + 16 * f + (lines & 7) == place).astype(jnp.bfloat16)
        placed = jnp.dot(chosen, normed, preferred_element_type=jnp.float32)
        upper = (iota((tall, half), 0) & 15) < 8
        placed = jnp.where(upper, placed[:, :half], placed[:, half:]).astype(jnp.bfloat16)
        outgoing_v[:, :, f * model_width :] = placed.reshape(n_seq, 16, half)

    a_copies = []
    for m in plane[::-1] + [0] + [m + 1 for m in plane[::-1]] + [1]:
        target = flip(my_seq, m)
        if m == 0:
            continue
        copy = pltpu.make_async_remote_copy(
            src_ref=outgoing_v.at[target],
            dst_ref=landed_ref.at[my_seq],
            send_sem=a_send.at[m - 1],
            recv_sem=a_recv.at[m - 1],
            device_id=(my_dp, target),
            device_id_type=MESH,
        )
        copy.start()
        a_copies.append(copy)
    keep = pltpu.make_async_copy(outgoing_v.at[my_seq], landed_ref.at[my_seq], local_sem.at[3])
    keep.start()
    for copy in z_copies + list(sent.values()):
        copy.wait_send()
    keep.wait()
    for copy in a_copies:
        copy.wait()


def layout_kernel(capacity, landed_ref, out_ref):
    n_seq, _, lanes = landed_ref.shape
    model_width = out_ref.shape[1] // 4
    half = model_width // 2
    block_rows = 4 * capacity
    out_rows = n_seq * capacity
    landed = landed_ref[...].reshape(n_seq * 16, lanes)
    rows = iota((out_rows, n_seq * 16), 0)
    lines = iota((out_rows, n_seq * 16), 1)
    full = block_rows // 16

    def pick(first, line, j, keep):
        spot = first + line
        return (
            (rows == (lines >> 4) * capacity + (spot >> 2)) & ((spot & 3) == j) & keep
        ).astype(jnp.bfloat16)

    always = lines >= 0
    for j in range(4):
        left = jnp.zeros((out_rows, half), jnp.float32)
        right = jnp.zeros((out_rows, half), jnp.float32)
        for f in range(full):
            part = jnp.dot(
                pick(16 * f, lines & 15, j, always),
                landed[:, f * model_width : (f + 1) * model_width],
                preferred_element_type=jnp.float32,
            )
            left, right = left + part[:, :half], right + part[:, half:]
        if block_rows % 16:
            tail = landed[:, full * model_width :]
            left = left + jnp.dot(
                pick(16 * full, lines & 7, j, (lines & 15) < 8), tail,
                preferred_element_type=jnp.float32,
            )
            right = right + jnp.dot(
                pick(16 * full, lines & 7, j, (lines & 15) >= 8), tail,
                preferred_element_type=jnp.float32,
            )
        out_ref[:, j * model_width : j * model_width + half] = left.astype(jnp.bfloat16)
        out_ref[:, j * model_width + half : (j + 1) * model_width] = right.astype(jnp.bfloat16)


def fused_body(patches, query_key_value, counts, owner_index, out_weight, ln_gain, ln_bias):
    row_count, model_width = patches.shape
    n_dp, n_seq = lax.axis_size("dp"), lax.axis_size("seq")
    capacity = max(2, (row_count // 4 + n_seq - 1) // n_seq)
    block_lanes = model_width * 4 * capacity // 16
    any_spec = pl.BlockSpec(memory_space=pl.ANY)
    vmem_spec = pl.BlockSpec(memory_space=pltpu.VMEM)
    dma = pltpu.SemaphoreType.DMA
    landed = pl.pallas_call(
        functools.partial(fused_kernel, n_dp, n_seq, capacity),
        out_shape=jax.ShapeDtypeStruct((n_seq, 16, block_lanes), jnp.bfloat16),
        in_specs=[
            any_spec, any_spec, pl.BlockSpec(memory_space=pltpu.SMEM), vmem_spec, any_spec,
            vmem_spec, vmem_spec,
        ],
        out_specs=vmem_spec,
        scratch_shapes=[
            pltpu.VMEM(patches.shape, jnp.bfloat16),
            pltpu.VMEM(query_key_value.shape, jnp.bfloat16),
            pltpu.VMEM((n_dp,) + out_weight.shape[::-1], jnp.bfloat16),
            pltpu.VMEM(patches.shape, jnp.bfloat16),
            pltpu.VMEM((n_dp, row_count, out_weight.shape[1]), jnp.float32),
            pltpu.VMEM((n_seq, 16, block_lanes), jnp.bfloat16),
            dma((4,)),
            dma((n_dp - 1,)), dma((n_dp,)),
            dma((n_dp - 1, 7)), dma((n_dp - 1, 7)),
            dma((n_seq - 1,)), dma((n_seq - 1,)),
        ],
        compiler_params=pltpu.CompilerParams(
            collective_id=0, has_side_effects=True
        ),
        name="fused",
    )(
        patches, query_key_value, counts, owner_index.T, out_weight.T,
        ln_gain, ln_bias,
    )
    return pl.pallas_call(
        functools.partial(layout_kernel, capacity),
        out_shape=jax.ShapeDtypeStruct((n_seq * capacity, 4 * model_width), jnp.bfloat16),
        in_specs=[vmem_spec],
        out_specs=vmem_spec,
        compiler_params=pltpu.CompilerParams(vmem_limit_bytes=16 * 1024 * 1024),
        name="layout",
    )(landed)


def body(patches, query_key_value, counts, owner_index, out_weight, ln_gain, ln_bias):
    n_seq = lax.axis_size("seq")
    square = n_seq == 2 * 2 * 2 and out_weight.shape[1] % (8 * n_seq) == 0
    run = fused_body if square else plain_body
    return run(patches, query_key_value, counts, owner_index, out_weight, ln_gain, ln_bias)


def solution(mesh):
    placed = (
        P(("dp", "seq"), None),
        P(("dp", "seq"), None),
        P(("dp", "seq"), None),
        P(("dp", "seq"), None),
        P(None, "dp"),
        P(),
        P(),
    )
    return jax.shard_map(
        body, mesh=mesh, in_specs=placed, out_specs=P(("dp", "seq"), None), check_vma=False
    )
```

```python
import functools

import jax
import jax.numpy as jnp
from jax import lax
from jax.experimental import pallas as pl
from jax.experimental.pallas import tpu as pltpu
from jax.sharding import PartitionSpec as P

HEADS = 16
IMGS = 4
MESH = pl.DeviceIdType.MESH


def segment_rows(count_row, row_count):
    image_ends = jnp.cumsum(count_row)
    row_ids = jnp.arange(row_count, dtype=jnp.int32)
    return jnp.sum((row_ids[:, None] >= image_ends[None, :]).astype(jnp.int32), axis=1)


def attend(packed, segment_ids, model_width):
    row_count = packed.shape[0]
    head_size = model_width // HEADS
    queries = packed[:, :model_width].reshape(row_count, HEADS, head_size)
    keys_all = packed[:, model_width : 2 * model_width].reshape(row_count, HEADS, head_size)
    values_all = packed[:, 2 * model_width :].reshape(row_count, HEADS, head_size)
    scores = jnp.einsum(
        "qhd,khd->hqk", queries, keys_all, preferred_element_type=jnp.float32
    ) * head_size ** (-0.5)
    same_image = segment_ids[:, None] == segment_ids[None, :]
    scores = jnp.where(same_image[None, :, :], scores, -1e30)
    top_score = jnp.max(scores, axis=2, keepdims=True)
    expo = jnp.exp(scores - top_score)
    attn_weights = (expo / jnp.sum(expo, axis=2, keepdims=True)).astype(jnp.bfloat16)
    context = jnp.einsum(
        "hqk,khd->qhd", attn_weights, values_all, preferred_element_type=jnp.float32
    )
    return context.reshape(row_count, model_width).astype(jnp.bfloat16)


def merge_and_place(hidden, segment_ids, owners, ln_gain, ln_bias, owner_count, capacity):
    row_count, model_width = hidden.shape
    row_mean = jnp.mean(hidden, axis=1, keepdims=True)
    centered = hidden - row_mean
    row_var = jnp.mean(centered * centered, axis=1, keepdims=True)
    normed = (centered * lax.rsqrt(row_var + 1e-06) * ln_gain[None, :] + ln_bias[None, :]).astype(
        jnp.bfloat16
    )
    merged = normed.reshape(row_count // 4, 4 * model_width)
    live_group = segment_ids.reshape(row_count // 4, 4)[:, 0] < IMGS
    group_ids = jnp.arange(row_count // 4, dtype=jnp.int32)
    earlier = (
        (owners[None, :] == owners[:, None])
        & (group_ids[None, :] < group_ids[:, None])
        & live_group[None, :]
    )
    slot_index = jnp.sum(earlier.astype(jnp.int32), axis=1)
    target = owners * capacity + slot_index
    slot_ids = jnp.arange(owner_count * capacity, dtype=jnp.int32)
    onehot_map = ((slot_ids[:, None] == target[None, :]) & live_group[None, :]).astype(jnp.bfloat16)
    return jnp.dot(onehot_map, merged, preferred_element_type=jnp.float32).astype(jnp.bfloat16)


def plain_body(patches, query_key_value, counts, owner_index, out_weight, ln_gain, ln_bias):
    row_count, model_width = patches.shape
    owner_count = lax.axis_size("seq")
    group_count = row_count // 4
    capacity = max(2, (group_count + owner_count - 1) // owner_count)
    segment_ids = segment_rows(counts[0], row_count)
    context = attend(query_key_value, segment_ids, model_width)
    slice_rows = model_width // owner_count
    own_slice = lax.dynamic_slice_in_dim(
        out_weight, lax.axis_index("seq") * slice_rows, slice_rows, 0
    )
    weight_slab = lax.all_gather(own_slice, "dp", axis=1, tiled=True)
    projected = jnp.dot(
        context,
        lax.all_gather(weight_slab, "seq", axis=0, tiled=True),
        preferred_element_type=jnp.float32,
    )
    hidden = patches.astype(jnp.float32) + projected
    outgoing = merge_and_place(
        hidden, segment_ids, owner_index[:, 0], ln_gain, ln_bias, owner_count, capacity
    )
    outgoing = outgoing.reshape(owner_count, capacity, 4 * model_width)
    received = lax.all_to_all(outgoing, "seq", split_axis=0, concat_axis=0, tiled=True)
    return received.reshape(owner_count * capacity, 4 * model_width)


def flip(index, mask):
    bit = 1
    while bit <= mask:
        if mask & bit:
            index = index + bit - 2 * bit * ((index // bit) % 2)
        bit *= 2
    return index


def iota(shape, dim):
    return lax.broadcasted_iota(jnp.int32, shape, dim)


def fused_kernel(
    n_dp, n_seq, capacity,
    patches_ref, packed_ref, counts_ref, owners_ref, weight_ref, gain_ref, bias_ref,
    landed_ref,
    patches_v, packed_v, weight_v, context_v, projected_v, outgoing_v,
    local_sem, z_send, z_recv, p_send, p_recv, a_send, a_recv,
):
    row_count, model_width = patches_ref.shape
    head_size = model_width // HEADS
    piece_rows = weight_ref.shape[0] // (n_seq // 2)
    piece_lanes = model_width // 2
    my_dp, my_seq = lax.axis_index("dp"), lax.axis_index("seq")
    plane = list(range(2, n_seq, 2))
    partner = flip(my_seq, 1)

    load_packed = pltpu.make_async_copy(packed_ref, packed_v, local_sem.at[0])
    load_patches = pltpu.make_async_copy(patches_ref, patches_v, local_sem.at[1])
    load_weight = pltpu.make_async_copy(weight_ref, weight_v.at[my_dp], local_sem.at[2])
    load_packed.start()
    load_weight.start()
    load_patches.start()

    barrier = pltpu.get_barrier_semaphore()
    for k in range(1, n_dp):
        pl.semaphore_signal(
            barrier, inc=1, device_id=(lax.rem(my_dp + k, n_dp), my_seq), device_id_type=MESH
        )
    for m in range(1, n_seq):
        pl.semaphore_signal(barrier, inc=1, device_id=(my_dp, flip(my_seq, m)), device_id_type=MESH)
    pl.semaphore_wait(barrier, n_dp + n_seq - 2)

    first_lanes = piece_lanes // 256 * 128

    def piece_of(ref, seq, part):
        skip = part * first_lanes
        width = piece_lanes - first_lanes if part else first_lanes
        return ref.at[
            pl.ds(pl.multiple_of((seq // 2) * piece_rows, piece_rows), piece_rows),
            pl.ds(pl.multiple_of((seq % 2) * piece_lanes + skip, 128), width),
        ]

    def at_dp(table):
        return sum(
            entry * (1 - ((my_dp - i + n_dp) % n_dp + n_dp - 1) // n_dp)
            for i, entry in enumerate(table)
        )

    orders = [
        sorted((e for e in range(n_dp) if e != d), key=lambda e: (abs(e - d), e))
        for d in range(n_dp)
    ]
    rounds = range(2 * (n_dp - 1))
    sources = [at_dp([order[r // 2] for order in orders]) for r in rounds]
    core = my_seq % 2
    x_side, y_side = flip(my_seq, 2), flip(my_seq, 4)
    side_a = (1 - core) * x_side + core * y_side
    side_b = core * x_side + (1 - core) * y_side
    far_side = flip(my_seq, 6)

    def z_copy(r, owner_dp):
        return pltpu.make_async_remote_copy(
            src_ref=piece_of(weight_ref, my_seq, r % 2),
            dst_ref=piece_of(weight_v.at[owner_dp], my_seq, r % 2),
            send_sem=z_send.at[r],
            recv_sem=z_recv.at[owner_dp, r % 2],
            device_id=(sources[r], my_seq),
            device_id_type=MESH,
        )

    z_copies = [z_copy(r, my_dp) for r in rounds]
    for copy in z_copies:
        copy.start()

    sent = {}

    def send_piece(r, kind, seq_of_rows, target):
        piece = piece_of(weight_v.at[sources[r]], seq_of_rows, r % 2)
        copy = pltpu.make_async_remote_copy(
            src_ref=piece, dst_ref=piece, send_sem=p_send.at[r, kind], recv_sem=p_recv.at[r, kind],
            device_id=(my_dp, target), device_id_type=MESH,
        )
        copy.start()
        sent[r, kind] = copy

    def from_z(r):
        z_copy(r, sources[r]).wait_recv()
        send_piece(r, 0, my_seq, side_a)
        send_piece(r, 1, my_seq, side_b)
        send_piece(r, 3, my_seq, partner)

    def from_sides(r):
        sent[r, 0].wait_recv()
        send_piece(r, 2, side_a, side_b)
        send_piece(r, 4, side_a, partner)
        sent[r, 1].wait_recv()
        send_piece(r, 5, side_b, partner)

    def from_far(r):
        sent[r, 2].wait_recv()
        send_piece(r, 6, far_side, partner)

    def project(dp):
        projected_v[dp] = lax.dot_general(
            context_v[...], weight_v[dp], (((1,), (1,)), ((), ())),
            preferred_element_type=jnp.float32,
        )

    def finish(r):
        for kind in range(3, 7):
            sent[r, kind].wait_recv()
        if r % 2:
            project(sources[r])

    load_packed.wait()
    ends, total = [], 0
    for i in range(IMGS):
        total = total + counts_ref[0, i]
        ends.append(total)

    def segments(shape, dim):
        ids = iota(shape, dim)
        found = jnp.zeros(shape, jnp.int32)
        for end in ends:
            found = found + (ids >= end).astype(jnp.int32)
        return found

    same = segments((row_count, row_count), 0) == segments((row_count, row_count), 1)
    scale = head_size ** (-0.5)
    pending = None
    pending_at = 0
    for head in range(HEADS):
        first, last = head * head_size, (head + 1) * head_size
        low, high = first // 128 * 128, -(-last // 128) * 128
        lanes = iota((row_count, high - low), 1)
        mine = (lanes >= first - low) & (lanes < last - low)
        queries = packed_v[:, low:high]
        queries = jnp.where(mine, queries, jnp.zeros_like(queries))
        scores = lax.dot_general(
            queries, packed_v[:, model_width + low : model_width + high],
            (((1,), (1,)), ((), ())), preferred_element_type=jnp.float32,
        )
        scores = jnp.where(same, scores, -1e30)
        top_score = jnp.max(scores, axis=1, keepdims=True)
        expo = jnp.exp((scores - top_score) * scale)
        weights = (expo * (1.0 / jnp.sum(expo, axis=1, keepdims=True))).astype(jnp.bfloat16)
        found = jnp.dot(
            weights, packed_v[:, 2 * model_width + low : 2 * model_width + high],
            preferred_element_type=jnp.float32,
        )
        found = jnp.where(mine, found, 0.0)
        if pending is not None and pending_at > low:
            shared = pending_at - low
            if shared > 0:
                head_part = pending + found[:, :shared]
                found = (
                    jnp.concatenate([head_part, found[:, shared:]], axis=1)
                    if shared < high - low else head_part
                )
        done = last // 128 * 128
        if done > low:
            context_v[:, low:done] = found[:, : done - low].astype(jnp.bfloat16)
        if done < high:
            pending, pending_at = found[:, done - low :], high
        else:
            pending = None

    load_weight.wait()
    project(my_dp)
    load_patches.wait()
    for step in range(len(rounds) + 3):
        if step < len(rounds):
            from_z(step)
        if 1 <= step <= len(rounds):
            from_sides(step - 1)
        if 2 <= step <= len(rounds) + 1:
            from_far(step - 2)
        if 3 <= step:
            finish(step - 3)
    hidden = patches_v[...].astype(jnp.float32) + jnp.concatenate(
        [projected_v[d] for d in range(n_dp)], axis=1
    )
    row_mean = jnp.mean(hidden, axis=1, keepdims=True)
    centered = hidden - row_mean
    row_var = jnp.mean(centered * centered, axis=1, keepdims=True)
    normed = (
        centered * lax.rsqrt(row_var + 1e-06) * gain_ref[...].reshape(1, model_width)
        + bias_ref[...].reshape(1, model_width)
    ).astype(jnp.bfloat16)

    group_count = row_count // 4
    diagonal = iota((group_count, group_count), 0) == iota((group_count, group_count), 1)
    owners = jnp.sum(jnp.where(diagonal, owners_ref[...], 0), axis=1, keepdims=True)
    groups = iota((group_count, row_count), 0)
    group_of_row = iota((group_count, row_count), 1) >> 2
    owner_of_row = jnp.sum(jnp.where(groups == group_of_row, owners, 0), axis=0, keepdims=True)
    earlier = (owners == owner_of_row) & (groups < group_of_row) & (groups * 4 < total)
    slot_of_row = jnp.sum(earlier.astype(jnp.int32), axis=0, keepdims=True)
    block_rows = 4 * capacity
    row_ids = iota((1, row_count), 1)
    place = owner_of_row * block_rows + slot_of_row * 4 + (row_ids & 3)
    place = jnp.where((row_ids >> 2) * 4 < total, place, -1)
    tall = n_seq * 16
    lines = iota((tall, row_count), 0)
    half = model_width // 2
    for f in range(block_rows // 16):
        chosen = ((lines >> 4) * block_rows + 16 * f + (lines & 15) == place).astype(jnp.bfloat16)
        placed = jnp.dot(chosen, normed, preferred_element_type=jnp.float32).astype(jnp.bfloat16)
        outgoing_v[:, :, f * model_width : (f + 1) * model_width] = placed.reshape(
            n_seq, 16, model_width
        )
    if block_rows % 16:
        f = block_rows // 16
        chosen = ((lines >> 4) * block_rows + 16 * f + (lines & 7) == place).astype(jnp.bfloat16)
        placed = jnp.dot(chosen, normed, preferred_element_type=jnp.float32)
        upper = (iota((tall, half), 0) & 15) < 8
        placed = jnp.where(upper, placed[:, :half], placed[:, half:]).astype(jnp.bfloat16)
        outgoing_v[:, :, f * model_width :] = placed.reshape(n_seq, 16, half)

    a_copies = []
    for m in plane[::-1] + [0] + [m + 1 for m in plane[::-1]] + [1]:
        target = flip(my_seq, m)
        if m == 0:
            continue
        copy = pltpu.make_async_remote_copy(
            src_ref=outgoing_v.at[target],
            dst_ref=landed_ref.at[my_seq],
            send_sem=a_send.at[m - 1],
            recv_sem=a_recv.at[m - 1],
            device_id=(my_dp, target),
            device_id_type=MESH,
        )
        copy.start()
        a_copies.append(copy)
    keep = pltpu.make_async_copy(outgoing_v.at[my_seq], landed_ref.at[my_seq], local_sem.at[3])
    keep.start()
    for copy in z_copies + list(sent.values()):
        copy.wait_send()
    keep.wait()
    for copy in a_copies:
        copy.wait()


def layout_kernel(capacity, landed_ref, out_ref):
    n_seq, _, lanes = landed_ref.shape
    model_width = out_ref.shape[1] // 4
    half = model_width // 2
    block_rows = 4 * capacity
    out_rows = n_seq * capacity
    landed = landed_ref[...].reshape(n_seq * 16, lanes)
    rows = iota((out_rows, n_seq * 16), 0)
    lines = iota((out_rows, n_seq * 16), 1)
    full = block_rows // 16

    def pick(first, line, j, keep):
        spot = first + line
        return (
            (rows == (lines >> 4) * capacity + (spot >> 2)) & ((spot & 3) == j) & keep
        ).astype(jnp.bfloat16)

    always = lines >= 0
    for j in range(4):
        left = jnp.zeros((out_rows, half), jnp.float32)
        right = jnp.zeros((out_rows, half), jnp.float32)
        for f in range(full):
            part = jnp.dot(
                pick(16 * f, lines & 15, j, always),
                landed[:, f * model_width : (f + 1) * model_width],
                preferred_element_type=jnp.float32,
            )
            left, right = left + part[:, :half], right + part[:, half:]
        if block_rows % 16:
            tail = landed[:, full * model_width :]
            left = left + jnp.dot(
                pick(16 * full, lines & 7, j, (lines & 15) < 8), tail,
                preferred_element_type=jnp.float32,
            )
            right = right + jnp.dot(
                pick(16 * full, lines & 7, j, (lines & 15) >= 8), tail,
                preferred_element_type=jnp.float32,
            )
        out_ref[:, j * model_width : j * model_width + half] = left.astype(jnp.bfloat16)
        out_ref[:, j * model_width + half : (j + 1) * model_width] = right.astype(jnp.bfloat16)


def fused_body(patches, query_key_value, counts, owner_index, out_weight, ln_gain, ln_bias):
    row_count, model_width = patches.shape
    n_dp, n_seq = lax.axis_size("dp"), lax.axis_size("seq")
    capacity = max(2, (row_count // 4 + n_seq - 1) // n_seq)
    block_lanes = model_width * 4 * capacity // 16
    any_spec = pl.BlockSpec(memory_space=pl.ANY)
    vmem_spec = pl.BlockSpec(memory_space=pltpu.VMEM)
    dma = pltpu.SemaphoreType.DMA
    landed = pl.pallas_call(
        functools.partial(fused_kernel, n_dp, n_seq, capacity),
        out_shape=jax.ShapeDtypeStruct((n_seq, 16, block_lanes), jnp.bfloat16),
        in_specs=[
            any_spec, any_spec, pl.BlockSpec(memory_space=pltpu.SMEM), vmem_spec, any_spec,
            vmem_spec, vmem_spec,
        ],
        out_specs=vmem_spec,
        scratch_shapes=[
            pltpu.VMEM(patches.shape, jnp.bfloat16),
            pltpu.VMEM(query_key_value.shape, jnp.bfloat16),
            pltpu.VMEM((n_dp,) + out_weight.shape[::-1], jnp.bfloat16),
            pltpu.VMEM(patches.shape, jnp.bfloat16),
            pltpu.VMEM((n_dp, row_count, out_weight.shape[1]), jnp.float32),
            pltpu.VMEM((n_seq, 16, block_lanes), jnp.bfloat16),
            dma((4,)),
            dma((2 * (n_dp - 1),)), dma((n_dp, 2)),
            dma((2 * (n_dp - 1), 7)), dma((2 * (n_dp - 1), 7)),
            dma((n_seq - 1,)), dma((n_seq - 1,)),
        ],
        compiler_params=pltpu.CompilerParams(
            collective_id=0, has_side_effects=True
        ),
        name="fused",
    )(
        patches, query_key_value, counts, owner_index.T, out_weight.T,
        ln_gain, ln_bias,
    )
    return pl.pallas_call(
        functools.partial(layout_kernel, capacity),
        out_shape=jax.ShapeDtypeStruct((n_seq * capacity, 4 * model_width), jnp.bfloat16),
        in_specs=[vmem_spec],
        out_specs=vmem_spec,
        compiler_params=pltpu.CompilerParams(vmem_limit_bytes=16 * 1024 * 1024),
        name="layout",
    )(landed)


def body(patches, query_key_value, counts, owner_index, out_weight, ln_gain, ln_bias):
    n_seq = lax.axis_size("seq")
    square = n_seq == 2 * 2 * 2 and out_weight.shape[1] % (8 * n_seq) == 0
    run = fused_body if square else plain_body
    return run(patches, query_key_value, counts, owner_index, out_weight, ln_gain, ln_bias)


def solution(mesh):
    placed = (
        P(("dp", "seq"), None),
        P(("dp", "seq"), None),
        P(("dp", "seq"), None),
        P(("dp", "seq"), None),
        P(None, "dp"),
        P(),
        P(),
    )
    return jax.shard_map(
        body, mesh=mesh, in_specs=placed, out_specs=P(("dp", "seq"), None), check_vma=False
    )
```
